256 devices in a mesh: region: 128 (over z_hi, x, y, core), split: 2 (over z_lo).
Axes of the slice: x: 4, y: 4, z: 8 (z_hi: 4, z_lo: 2; z = z_hi * 2 + z_lo), core: 2. Of those that a mesh axis runs over, the one named last changes fastest.
Arguments:
- features: bfloat16 [96, 131072], P(None, ('region', 'split')), may hold values from -6 to 6
- kernel_one: bfloat16 [27, 96, 96], replicated, may hold values from -0.125 to 0.125
- kernel_two: bfloat16 [27, 96, 192], replicated, may hold values from -0.125 to 0.125
- occupancy: int32 [256, 512], P(('region', 'split')), may hold values 0 or 1
- neighbors: int32 [256, 27], P(('region', 'split')), may hold values from -1 to 255, as said below
- cotangent: bfloat16 [192, 131072], P(None, ('region', 'split')), may hold values from -0.016479492 to 0.016479492
Outputs:
- output: bfloat16 [192, 131072], P(None, ('region', 'split'))
- grad_one: float32 [27, 96, 96], replicated
- grad_two: float32 [27, 96, 192], replicated
The draws below stay inside these ranges and needn't reach their ends.
Inputs may be any that keep to these rules, and one draw needn't show every extreme that they name: `neighbors`: entry k = 9 (dx + 1) + 3 (dy + 1) + (dz + 1) of a block's row is the active block whose block coordinates differ by (dx, dy, dz), or -1 if there is none; entry 13 is the block itself. Blocks are numbered in device order. The blocks of region r have x coordinate r and y coordinate 0 or 1; the device of split index s holds the blocks with z coordinate s. So a neighbour in region r - 1 or r + 1 differs by dx = -1 or +1, and a neighbour on the other device of the same region lies across the z boundary between the two halves.
All inputs are finite; a program needn't handle non-finite values. No bound on the sum of `occupancy` on one device may be relied on, other than what follows from the above.
Results may differ from the reference program's by a relative error of at most 0.0049.
Values may be sent and summed in bfloat16 or wider, within the bound.
A program may use at most 64 MiB of HBM per device.

```python
import jax
import jax.numpy as jnp
import numpy as np
from jax import lax

C1 = 96
C2 = 192
B_DEV = 1
BLOCKS = 256


def draw_neighbors(key, part):
    device_count = BLOCKS // B_DEV
    regions = device_count // 2
    cell_count = 2 * B_DEV
    scores = jax.random.randint(key, (device_count, cell_count), 0, 1 << 20) * cell_count + jnp.arange(cell_count)[None, :]
    picked = jnp.sort(jnp.argsort(scores, axis=1)[:, :B_DEV], axis=1).astype(jnp.int32)
    device_ids = jnp.arange(device_count, dtype=jnp.int32)[:, None]
    coord_x = jnp.broadcast_to(device_ids // 2, (device_count, B_DEV)).reshape(-1)
    coord_y = (picked // B_DEV).reshape(-1)
    coord_z = (device_ids % 2 * B_DEV + picked % B_DEV).reshape(-1)
    block_ids = jnp.arange(BLOCKS, dtype=jnp.int32)
    cell_grid = jnp.full((regions, 2, 2 * B_DEV), -1, jnp.int32).at[coord_x, coord_y, coord_z].set(block_ids)
    offsets = jnp.arange(27, dtype=jnp.int32)
    target_x = coord_x[:, None] + offsets[None, :] // 9 - 1
    target_y = coord_y[:, None] + offsets[None, :] // 3 % 3 - 1
    target_z = coord_z[:, None] + offsets[None, :] % 3 - 1
    inside = (target_x >= 0) & (target_x < regions) & (target_y >= 0) & (target_y < 2) & (target_z >= 0) & (target_z < 2 * B_DEV)
    located = cell_grid[jnp.clip(target_x, 0, regions - 1), jnp.clip(target_y, 0, 1), jnp.clip(target_z, 0, 2 * B_DEV - 1)]
    return jnp.where(inside, located, -1).astype(jnp.int32)


def touch_ends(entries, own_key, smallest, high):
    extent = entries.shape
    spot = [jax.random.randint(jax.random.fold_in(own_key, axis), (), 0, extent[axis]) for axis in range(len(extent))]
    entries = entries.at[tuple(spot)].set(smallest)
    longest = extent.index(max(extent))
    spot[longest] = (spot[longest] + 1) % extent[longest]
    return entries.at[tuple(spot)].set(high)


def level_of(own_key, extent, split, least, high):
    factor_of = 1.0
    for dim, blocks in split:
        draws = jax.random.uniform(jax.random.fold_in(jax.random.fold_in(own_key, 6), dim), (blocks,), jnp.float32, least / len(split), high / len(split))
        factor_of = factor_of * jnp.repeat(jnp.exp(draws), extent[dim] // blocks).reshape((-1,) + (1,) * (len(extent) - 1 - dim))
    return factor_of


def centred(stream_key, dims, spread, reach, shards=(), held_as=jnp.bfloat16):
    factor_of = level_of(stream_key, dims, shards, -0.22, 0.18) if shards else 1.0
    values = jax.random.normal(stream_key, dims, jnp.float32) * spread * factor_of
    return jnp.minimum(jnp.maximum(values, -reach), reach).astype(held_as)


def setup_inputs(seed: int = 0) -> dict:
    splits = jax.random.split(jax.random.key(seed), 7)
    return {
        "features": centred(splits[0], (C1, BLOCKS * 512), 1.0, 6.0, ((1, 256),)),
        "kernel_one": centred(splits[1], (27, C1, C1), (27 * C1) ** -0.5, 0.125),
        "kernel_two": centred(splits[2], (27, C1, C2), (27 * C1) ** -0.5, 0.125),
        "occupancy": touch_ends((jax.random.randint(splits[3], (BLOCKS, 512), 0, 5) < 3).astype(jnp.int32), jax.random.fold_in(splits[3], 1), 0, 1),
        "neighbors": draw_neighbors(jax.random.fold_in(splits[6], 71), 0),
        "cotangent": centred(splits[5], (C2, BLOCKS * 512), ((BLOCKS * 512) ** -0.5), 0.016479492, ((1, 256),)),
    }


def voxel_tables():
    voxels = np.arange(512)
    along_x = voxels // 64
    along_y = (voxels // 8) % 8
    along_z = voxels % 8
    block_code = np.zeros((27, 512), np.int32)
    voxel_code = np.zeros((27, 512), np.int32)
    for offset in range(27):
        moved_x = along_x + offset // 9 - 1
        moved_y = along_y + (offset // 3) % 3 - 1
        moved_z = along_z + offset % 3 - 1
        block_code[offset] = (moved_x // 8 + 1) * 9 + (moved_y // 8 + 1) * 3 + (moved_z // 8 + 1)
        voxel_code[offset] = (moved_x % 8) * 64 + (moved_y % 8) * 8 + moved_z % 8
    return block_code, voxel_code


def convolve(window, lookup, kernel):
    def accumulate(offset, total):
        picked = jnp.take(window, lax.dynamic_index_in_dim(lookup, offset, 0, keepdims=False), axis=1).astype(jnp.float32)
        weights = lax.dynamic_index_in_dim(kernel, offset, 0, keepdims=False).astype(jnp.float32)
        return total + jnp.dot(weights.T, picked, precision=lax.Precision.HIGHEST)
    return lax.fori_loop(0, 27, accumulate, jnp.zeros((kernel.shape[2], lookup.shape[1]), jnp.float32))


def kernel_gradient(window, lookup, gradient):
    gradient_wide = gradient.astype(jnp.float32)

    def accumulate(offset, total):
        picked = jnp.take(window, lax.dynamic_index_in_dim(lookup, offset, 0, keepdims=False), axis=1).astype(jnp.float32)
        product = jnp.dot(picked, gradient_wide.T, precision=lax.Precision.HIGHEST)
        return lax.dynamic_update_index_in_dim(total, product, offset, 0)
    return lax.fori_loop(0, 27, accumulate, jnp.zeros((27, window.shape[0], gradient.shape[0]), jnp.float32))


def convolve_back(window, lookup, kernel):
    def accumulate(offset, total):
        picked = jnp.take(window, lax.dynamic_index_in_dim(lookup, 26 - offset, 0, keepdims=False), axis=1).astype(jnp.float32)
        weights = lax.dynamic_index_in_dim(kernel, offset, 0, keepdims=False).astype(jnp.float32)
        return total + jnp.dot(weights, picked, precision=lax.Precision.HIGHEST)
    return lax.fori_loop(0, 27, accumulate, jnp.zeros((kernel.shape[1], lookup.shape[1]), jnp.float32))


def padded(values):
    return jnp.concatenate([values, jnp.zeros((values.shape[0], 1), values.dtype)], axis=1)


def reference(features, kernel_one, kernel_two, occupancy, neighbors, cotangent):
    tables = voxel_tables()
    columns = features.shape[1]
    block_ids = jnp.transpose(jnp.take(neighbors, jnp.asarray(tables[0]), axis=1), (1, 0, 2))
    voxel_target = jnp.asarray(tables[1])[:, None, :]
    lookup = jnp.where(block_ids < 0, columns, block_ids * 512 + voxel_target).reshape(27, -1).astype(jnp.int32)
    active = (occupancy.reshape(-1) > 0)[None, :]
    zero_value = jnp.zeros((), features.dtype)
    masked = jnp.where(active, features, zero_value)
    hidden_pre = jnp.where(active, convolve(padded(masked), lookup, kernel_one), 0.0)
    hidden = jnp.where(active, jax.nn.silu(hidden_pre), 0.0).astype(jnp.bfloat16)
    output = jnp.where(active, convolve(padded(hidden), lookup, kernel_two), 0.0)
    grad_out = jnp.where(active, cotangent, zero_value)
    grad_two = kernel_gradient(padded(hidden), lookup, grad_out)
    back = convolve_back(padded(grad_out), lookup, kernel_two)
    sigmoid_pre = jax.nn.sigmoid(hidden_pre)
    grad_pre = jnp.where(active, back * sigmoid_pre * (1.0 + hidden_pre * (1.0 - sigmoid_pre)), 0.0).astype(jnp.bfloat16)
    grad_one = kernel_gradient(padded(masked), lookup, grad_pre)
    return (output.astype(jnp.bfloat16), grad_one, grad_two)
```

```python
import jax
import jax.numpy as jnp
import numpy as np
from jax import lax
from jax.experimental import pallas as pl
from jax.experimental.pallas import tpu as pltpu
from jax.sharding import PartitionSpec as P

MESH = pl.DeviceIdType.MESH
F32 = jnp.float32
BF16 = jnp.bfloat16
C1, C2 = 96, 192
K9 = 9 * C1
SEGS = (1024, 2048)
NCOPY = 5 + 5 + 2 * 34


def one_hots():
    faces = np.zeros((512, 128), np.float32)
    for x in range(8):
        for y in range(8):
            faces[x * 64 + y * 8 + 7, x * 8 + y] = 1
            faces[x * 64 + y * 8, 64 + x * 8 + y] = 1
    rim = [(y, z) for y in range(-1, 9) for z in range(-1, 9) if not (0 <= y < 8 and 0 <= z < 8)]
    rim_lane = {pos: i for i, pos in enumerate(rim)}

    columns = [(xp, y, z) for xp in (-1, 8) for y in range(8) for z in range(8)]
    for planes in (range(-1, 9), range(0, 8)):
        for xp in planes:
            columns += [(xp,) + pos for pos in rim] + [None] * (64 - len(rim))
    place = np.zeros((384, 1280), np.float32)
    offsets = np.zeros((27, 1280), np.float32)
    for n, pos in enumerate(columns):
        if pos is None:
            continue
        xp, y, z = pos
        ex, ey, ez = xp // 8, y // 8, z // 8
        if ex == 0 and ez == 0:
            continue
        offsets[9 * (ex + 1) + 3 * (ey + 1) + ez + 1, n] = 1
        if ex == 0:
            place[256 + (0 if ez < 0 else 64) + xp * 8 + y % 8, n] = 1
        else:
            place[(0 if ez == 0 else 128) + (0 if ex > 0 else 64) + (y % 8) * 8 + z % 8, n] = 1

    shifts = np.zeros((5, 256, 256), np.float32)
    for m in range(9):
        dy, dz = m // 3 - 1, m % 3 - 1
        for half in range(2):
            for y in range(8):
                for z in range(8):
                    col = (m % 2) * 128 + half * 64 + y * 8 + z
                    py, pz = y + dy, z + dz
                    if 0 <= py < 8 and 0 <= pz < 8:
                        row = half * 64 + py * 8 + pz
                    else:
                        row = 128 + half * 64 + rim_lane[(py, pz)]
                    shifts[m // 2, row, col] = 1
    return faces, place, offsets, shifts


def nt_dot(a, b):
    return lax.dot_general(a, b, (((1,), (1,)), ((), ())), preferred_element_type=F32)


def tn_dot(a, b):
    return lax.dot_general(a, b, (((0,), (0,)), ((), ())), preferred_element_type=F32)


def dot(a, b):
    return jnp.dot(a, b, preferred_element_type=F32)


def below(rows, lane):
    return lax.broadcasted_iota(jnp.int32, (rows, 128), 1) < lane


def main_kernel(
    feat_ref, k1_ref, k2_ref, k2b_ref, occ_ref, nb_ref, cot_ref, faces_ref, place_ref, offs_ref, shift_ref,
    out_ref, full1_ref, full2_ref,
    send_a, recv_a, send_h, recv_h, src1, src2, ev1, od1, ev2, od2, evg, odg,
    pk1, pk2, sb1, sb2, rb1, rb2, b11, b12, r11, r12, b21, b22, r21, r22, t21, t22, b31, b32, r31, r32,
    z1, z2, f1, f2, send_sem, recv_sem, out_sem,
):
    reg = lax.axis_index("region")
    s = lax.axis_index("split")
    core = lax.rem(reg, 2)
    y = lax.rem(lax.div(reg, 2), 4)
    x = lax.rem(lax.div(reg, 8), 4)
    zh = lax.div(reg, 32)
    z = zh * 2 + s

    def dev(core_, x_, y_, z_):
        return (((lax.div(z_, 2) * 4 + x_) * 4 + y_) * 2 + core_, lax.rem(z_, 2))

    m1 = x + (y - x) * core
    m2 = y + (x - y) * core
    m1_other = y + (x - y) * core
    partner = dev(1 - core, x, y, z)

    def along1(v):
        return dev(core, x + (v - x) * (1 - core), y + (v - y) * core, z)

    def along2(v):
        return dev(core, x + (v - x) * core, y + (v - y) * (1 - core), z)

    def along_z(v):
        return dev(core, x, y, v)

    up, down = lax.rem(reg + 1, 128), lax.rem(reg + 127, 128)
    halo_peers = ((up, s), (down, s), (up, 1 - s), (down, 1 - s), (reg, 1 - s))

    barrier = pltpu.get_barrier_semaphore()
    peers = list(halo_peers) + [partner]
    peers += [along1(lax.rem(m1 + d, 4)) for d in range(1, 4)]
    peers += [along2(lax.rem(m2 + d, 4)) for d in range(1, 4)]
    peers += [along_z(lax.rem(z + d, 8)) for d in range(1, 8)]
    for peer in peers:
        pl.semaphore_signal(barrier, inc=1, device_id=peer, device_id_type=MESH)

    started = []

    def copy(src, dst, i, peer):
        c = pltpu.make_async_remote_copy(
            src_ref=src, dst_ref=dst, send_sem=send_sem.at[i], recv_sem=recv_sem.at[i],
            device_id=peer, device_id_type=MESH,
        )
        c.start()
        started.append(c)
        return c

    active = (occ_ref[...] > 0).astype(F32)
    masked = (feat_ref[...].astype(F32) * active).astype(BF16)
    grad_out = (cot_ref[...].astype(F32) * active).astype(BF16)

    def send_tiles(own, channels, ref, first):
        tile_x = jnp.where(
            below(channels, 64), own[:, 0:128].astype(F32), own[:, 384:512].astype(F32)
        ).astype(BF16)
        ref[0, first : first + channels, :] = tile_x
        ref[1, first : first + channels, :] = dot(own, faces_ref[...]).astype(BF16)

    send_tiles(masked, C1, send_a, 0)
    send_tiles(grad_out, C2, send_a, C1)
    present = (jnp.broadcast_to(nb_ref[...], (16, 27)) >= 0).astype(F32).astype(BF16)
    flags = dot(present, offs_ref[...])[0:1, :]

    pl.semaphore_wait(barrier, len(peers))

    def send_halo(ref, into, base):
        order = (1, 0, 3, 2, 4)
        return [
            copy(ref.at[0 if q < 4 else 1], into.at[order[q]], base + order[q], halo_peers[q])
            for q in range(5)
        ]

    halo_a = send_halo(send_a, recv_a, 0)

    def gather(own, channels, recv, first, src, even, odd):
        lo = below(channels, 64)
        rows = slice(first, first + channels)

        def joined(p, q):
            return jnp.where(lo, recv[p, rows, :].astype(F32), recv[q, rows, :].astype(F32)).astype(BF16)

        raw = jnp.concatenate([joined(0, 1), joined(2, 3), recv[4, rows, :]], axis=1)
        halo = dot(raw, place_ref[...]) * flags
        ends = halo[:, 0:128]
        halo = halo.astype(BF16)
        rolled = pltpu.roll(own.astype(F32), 64, 1)
        for j in range(9):
            t = j // 2
            if j % 2:
                inner = own[:, t * 128 : (t + 1) * 128]
                rim = halo[:, 768 + t * 128 : 896 + t * 128]
            else:
                if t == 0:
                    inner = jnp.where(lo, ends, rolled[:, 0:128])
                elif t == 4:
                    inner = jnp.where(lo, rolled[:, 0:128], ends)
                else:
                    inner = rolled[:, t * 128 : (t + 1) * 128]
                inner = inner.astype(BF16)
                rim = halo[:, 128 + t * 128 : 256 + t * 128]
            src[j * channels : (j + 1) * channels, 0:128] = inner
            src[j * channels : (j + 1) * channels, 128:256] = rim

        def step(i, carry):
            moved = dot(src[0 : 9 * channels, :], shift_ref[i]).astype(BF16)
            for half in range(2):
                at = pl.ds(pl.multiple_of((2 * i + half) * channels, channels), channels)
                for j in range(9):
                    piece = moved[j * channels : (j + 1) * channels, half * 128 : (half + 1) * 128]
                    t = j // 2
                    if j % 2:
                        even[at, t * 128 : (t + 1) * 128] = piece
                    else:
                        odd[at, t * 128 : (t + 1) * 128] = piece
            return carry

        lax.fori_loop(0, 5, step, 0)

    def group(even, odd, rows, dx):
        if dx == 1:
            return even[rows, :]
        return odd[rows, 0:512] if dx == 0 else odd[rows, 128:640]

    first9 = slice(0, K9)

    def convolve(k_ref, even, odd):
        total = tn_dot(k_ref[0:K9, :], group(even, odd, first9, 0))
        total += tn_dot(k_ref[K9 : 2 * K9, :], group(even, odd, first9, 1))
        total += tn_dot(k_ref[2 * K9 : 3 * K9, :], group(even, odd, first9, 2))
        return total * active

    for c in halo_a:
        c.wait_recv()
    gather(masked, C1, recv_a, 0, src1, ev1, od1)
    hidden_pre = convolve(k1_ref, ev1, od1)
    sig = jax.nn.sigmoid(hidden_pre)
    hidden = (hidden_pre * sig).astype(BF16)
    send_tiles(hidden, C1, send_h, 0)
    halo_h = send_halo(send_h, recv_h, 5)

    gather(grad_out, C2, recv_a, C1, src2, evg, odg)
    back = jnp.zeros((C1, 512), F32)
    for dx in range(3):
        for m in range(9):
            back += dot(k2b_ref[26 - 9 * dx - m], group(evg, odg, slice(m * C2, (m + 1) * C2), dx))
    grad_pre = back * sig * (1.0 + hidden_pre * (1.0 - sig)) * active
    grad_pre = jnp.concatenate([grad_pre, jnp.zeros((32, 512), F32)], axis=0).astype(BF16)
    lo1296 = below(1296, 64)

    grad = jnp.concatenate(
        [nt_dot(group(ev1, od1, first9, dx), grad_pre) for dx in range(3)], axis=0
    )
    pk1[0:1296, :] = jnp.where(lo1296, grad[0:1296], pltpu.roll(grad[1296:2592], 64, 1))
    lane = lax.broadcasted_iota(jnp.int32, (648, 128), 1)
    rest = pltpu.roll(grad[0:648], 64, 1)
    for q in range(1, 4):
        rest = jnp.where(lane < 32 * q, rest, pltpu.roll(grad[648 * q : 648 * (q + 1)], (32 * q + 64) % 128, 1))
    pk1[1296:1944, :] = rest
    pk1[1944:2048, :] = jnp.zeros((104, 128), F32)

    def reduce_steps(h, base, pk, sb, rb, b1, r1, b2, r2, t2, b3, r3, zg, full):
        q1, q2, q3 = h // 4, h // 16, h // 128
        order = (2, 1, 3, 0)
        half = pl.ds(pl.multiple_of((1 - core) * h, h), h)
        sb[...] = pk[half, :].astype(BF16).reshape(4, q1, 128)
        first = []
        for n, d in enumerate(order):
            v = lax.rem(m1_other + d, 4)
            first.append(copy(sb.at[v], rb.at[n], base + n, partner))
        yield
        own = None
        second = []
        for n, d in enumerate(order):
            first[n].wait_recv()
            v = lax.rem(m1 + d, 4)
            part = pk[pl.ds(pl.multiple_of(core * h + v * q1, q1), q1), :] + rb[n].astype(F32)
            if d:
                b1[d - 1] = part.astype(BF16)
                second.append(copy(b1.at[d - 1], r1.at[d - 1], base + 3 + d, along1(v)))
            else:
                own = part
        yield
        for c in second:
            c.wait_recv()
        own = own + r1[0].astype(F32) + r1[1].astype(F32) + r1[2].astype(F32)
        b2[...] = own.reshape(4, q2, 128)
        third = []
        for d in (2, 1, 3):
            v = lax.rem(m2 + d, 4)
            t2[d - 1] = b2[v].astype(BF16)
            third.append(copy(t2.at[d - 1], r2.at[d - 1], base + 6 + d, along2(v)))
        yield
        for c in third:
            c.wait_recv()
        own = b2[m2] + r2[0].astype(F32) + r2[1].astype(F32) + r2[2].astype(F32)
        b3[...] = own.reshape(8, q3, 128)
        fourth = []
        for d in (4, 3, 5, 2, 6, 1, 7):
            v = lax.rem(z + d, 8)
            fourth.append(copy(b3.at[v], r3.at[d - 1], base + 9 + d, along_z(v)))
        yield
        for c in fourth:
            c.wait_recv()
        own = b3[z]
        for d in range(7):
            own = own + r3[d]
        zg[z] = own
        fifth = []
        for d in (4, 3, 5, 2, 6, 1, 7):
            v = lax.rem(z + d, 8)
            fifth.append(copy(zg.at[z], zg.at[z], base + 16 + d, along_z(v)))
        yield
        for c in fifth:
            c.wait_recv()
        full[core, m1, m2] = zg[...].reshape(q2, 128).astype(BF16)
        sixth = []
        for d in (2, 1, 3):
            v = lax.rem(m2 + d, 4)
            sixth.append(copy(full.at[core, m1, m2], full.at[core, m1, m2], base + 23 + d, along2(v)))
        yield
        for c in sixth:
            c.wait_recv()
        seventh = []
        for d in (2, 1, 3):
            v = lax.rem(m1 + d, 4)
            seventh.append(copy(full.at[core, m1], full.at[core, m1], base + 26 + d, along1(v)))
        eighth = [copy(full.at[core, m1], full.at[core, m1], base + 30, partner)]
        yield
        for n, d in ((1, 1), (2, 3), (0, 2)):
            seventh[n].wait_recv()
            v = lax.rem(m1 + 4 - d, 4)
            eighth.append(copy(full.at[core, v], full.at[core, v], base + 30 + d, partner))
        yield
        for c in eighth:
            c.wait_recv()
        yield

    red1 = reduce_steps(SEGS[0], 10, pk1, sb1, rb1, b11, r11, b21, r21, t21, b31, r31, z1, f1)
    next(red1)

    for c in halo_h:
        c.wait_recv()
    gather(hidden, C1, recv_h, 0, src1, ev2, od2)
    next(red1)
    grad = jnp.concatenate(
        [nt_dot(group(ev2, od2, first9, dx), grad_out) for dx in range(3)], axis=0
    )
    pk2[0:2592, :] = grad[:, 0:128]
    tail = jnp.concatenate([grad[:, 128:192], jnp.zeros((2592, 64), F32)], axis=1)
    pk2[2592:3888, :] = jnp.where(lo1296, tail[0:1296], pltpu.roll(tail[1296:2592], 64, 1))
    pk2[3888:4096, :] = jnp.zeros((208, 128), F32)

    red2 = reduce_steps(SEGS[1], 44, pk2, sb2, rb2, b12, r12, b22, r22, t22, b32, r32, z2, f2)
    next(red2)
    next(red1)
    next(red2)
    next(red1)
    out_ref[...] = convolve(k2_ref, ev2, od2).astype(BF16)
    next(red2)
    next(red1)
    next(red2)
    next(red1)
    next(red2)
    next(red1)
    next(red2)
    next(red1)
    next(red2)
    next(red1)
    save1 = pltpu.make_async_copy(f1, full1_ref, out_sem.at[0])
    save1.start()
    next(red2)
    next(red2)
    save2 = pltpu.make_async_copy(f2, full2_ref, out_sem.at[1])
    save2.start()
    for c in started:
        c.wait_send()
    save1.wait()
    save2.wait()


def unpack_kernel(p1_ref, p2_ref, o_ref, g1_ref, g2_ref, out_ref):
    out_ref[...] = o_ref[...]
    g2_ref[:, 0:128] = p2_ref[0:2592, :].astype(F32)
    fold = p2_ref[2592:3888, :].astype(F32)
    g2_ref[0:1296, 128:192] = fold[:, 0:64]
    g2_ref[1296:2592, 128:192] = pltpu.roll(fold, 64, 1)[:, 0:64]
    fold = p1_ref[0:1296, :].astype(F32)
    rest = p1_ref[1296:1944, :].astype(F32)
    both = (fold, pltpu.roll(fold, 64, 1))
    lo = below(648, 64)
    for q in range(4):
        left = both[q // 2][(q % 2) * 648 : (q % 2 + 1) * 648]
        right = pltpu.roll(rest, (64 - 32 * q) % 128, 1)
        g1_ref[648 * q : 648 * (q + 1), :] = jnp.where(lo, left, right)[:, 0:96]


def shards(features, kernel_one, kernel_two, occupancy, neighbors, cotangent):
    faces, place, offsets, shifts = (jnp.asarray(a, BF16) for a in one_hots())
    vmem = pl.BlockSpec(memory_space=pltpu.VMEM)

    def reduce_scratch(h):
        q1, q2, q3 = h // 4, h // 16, h // 128
        return [
            pltpu.VMEM((2 * h, 128), F32),
            pltpu.VMEM((4, q1, 128), BF16),
            pltpu.VMEM((4, q1, 128), BF16),
            pltpu.VMEM((3, q1, 128), BF16),
            pltpu.VMEM((3, q1, 128), BF16),
            pltpu.VMEM((4, q2, 128), F32),
            pltpu.VMEM((3, q2, 128), BF16),
            pltpu.VMEM((3, q2, 128), BF16),
            pltpu.VMEM((8, q3, 128), F32),
            pltpu.VMEM((7, q3, 128), F32),
            pltpu.VMEM((8, q3, 128), F32),
            pltpu.VMEM((2, 4, 4, q2, 128), BF16),
        ]

    pairs = zip(reduce_scratch(SEGS[0]), reduce_scratch(SEGS[1]))
    rows = 10 * C1
    scratch = [
        pltpu.VMEM((2, C1 + C2, 128), BF16),
        pltpu.VMEM((5, C1 + C2, 128), BF16),
        pltpu.VMEM((2, C1, 128), BF16),
        pltpu.VMEM((5, C1, 128), BF16),
        pltpu.VMEM((9 * C1, 256), BF16),
        pltpu.VMEM((9 * C2, 256), BF16),
        pltpu.VMEM((rows, 512), BF16),
        pltpu.VMEM((rows, 640), BF16),
        pltpu.VMEM((rows, 512), BF16),
        pltpu.VMEM((rows, 640), BF16),
        pltpu.VMEM((2 * rows, 512), BF16),
        pltpu.VMEM((2 * rows, 640), BF16),
        *(ref for pair in pairs for ref in pair),
        pltpu.SemaphoreType.DMA((NCOPY,)),
        pltpu.SemaphoreType.DMA((NCOPY,)),
        pltpu.SemaphoreType.DMA((2,)),
    ]
    out, full1, full2 = pl.pallas_call(
        main_kernel,
        out_shape=(
            jax.ShapeDtypeStruct((C2, 512), BF16),
            jax.ShapeDtypeStruct((2, 4, 4, SEGS[0] // 16, 128), BF16),
            jax.ShapeDtypeStruct((2, 4, 4, SEGS[1] // 16, 128), BF16),
        ),
        in_specs=[vmem] * 11,
        out_specs=(vmem, pl.BlockSpec(memory_space=pl.ANY), pl.BlockSpec(memory_space=pl.ANY)),
        scratch_shapes=scratch,
        compiler_params=pltpu.CompilerParams(
            collective_id=0, has_side_effects=True, vmem_limit_bytes=60 * 1024 * 1024
        ),
        name="sparse_conv",
    )(
        features, kernel_one.reshape(27 * C1, C1), kernel_two.reshape(27 * C1, C2), kernel_two,
        occupancy, neighbors, cotangent, faces, place, offsets, shifts,
    )
    grad_one, grad_two, out = pl.pallas_call(
        unpack_kernel,
        out_shape=(
            jax.ShapeDtypeStruct((27 * C1, C1), F32),
            jax.ShapeDtypeStruct((27 * C1, C2), F32),
            jax.ShapeDtypeStruct((C2, 512), BF16),
        ),
        in_specs=[vmem] * 3,
        out_specs=[vmem] * 3,
        name="unpack",
    )(full1.reshape(2 * SEGS[0], 128), full2.reshape(2 * SEGS[1], 128), out)
    return (out, grad_one.reshape(27, C1, C1), grad_two.reshape(27, C1, C2))


def solution(mesh):
    in_specs = (
        P(None, ("region", "split")),
        P(),
        P(),
        P(("region", "split"), None),
        P(("region", "split"), None),
        P(None, ("region", "split")),
    )
    out_specs = (P(None, ("region", "split")), P(), P())
    return jax.shard_map(shards, mesh=mesh, in_specs=in_specs, out_specs=out_specs, check_vma=False)
```

```python
import jax
import jax.numpy as jnp
import numpy as np
from jax import lax
from jax.experimental import pallas as pl
from jax.experimental.pallas import tpu as pltpu
from jax.sharding import PartitionSpec as P

MESH = pl.DeviceIdType.MESH
F32 = jnp.float32
BF16 = jnp.bfloat16
C1, C2 = 96, 192
K9 = 9 * C1
SEGS = (1024, 2048)
VMEM_MIB = 36
NCOPY = 5 + 5 + 2 * 34


def one_hots():
    faces = np.zeros((2, 512, 384), np.float32)
    for split in range(2):
        z = 7 - 7 * split
        for y in range(8):
            for x in range(8):
                for copy in range(2):
                    faces[split, x * 64 + y * 8 + z, copy * 64 + x * 8 + y] = 1
            for copy in range(12):
                faces[split, y * 8 + z, 128 + copy * 8 + y] = 1
                faces[split, 448 + y * 8 + z, 256 + copy * 8 + y] = 1
    rim = [(y, z) for y in range(-1, 9) for z in range(-1, 9) if not (0 <= y < 8 and 0 <= z < 8)]
    rim_lane = {pos: i for i, pos in enumerate(rim)}

    columns = [(xp, y, z) for xp in (-1, 8) for y in range(8) for z in range(8)]
    for planes in (range(-1, 9), range(0, 8)):
        for xp in planes:
            columns += [(xp,) + pos for pos in rim] + [None] * (64 - len(rim))
    place = np.zeros((256, 1280), np.float32)
    offsets = np.zeros((27, 1280), np.float32)
    for n, pos in enumerate(columns):
        if pos is None:
            continue
        xp, y, z = pos
        ex, ey, ez = xp // 8, y // 8, z // 8
        if ex == 0 and ez == 0:
            continue
        offsets[9 * (ex + 1) + 3 * (ey + 1) + ez + 1, n] = 1
        if ex == 0:
            place[128 + xp * 8 + y % 8, n] = 1
        elif ez == 0:
            place[(0 if ex > 0 else 64) + (y % 8) * 8 + z, n] = 1
        else:
            place[192 + (0 if ex > 0 else 8) + y % 8, n] = 1

    shifts = np.zeros((5, 256, 256), np.float32)
    for m in range(9):
        dy, dz = m // 3 - 1, m % 3 - 1
        for half in range(2):
            for y in range(8):
                for z in range(8):
                    col = (m % 2) * 128 + half * 64 + y * 8 + z
                    py, pz = y + dy, z + dz
                    if 0 <= py < 8 and 0 <= pz < 8:
                        row = half * 64 + py * 8 + pz
                    else:
                        row = 128 + half * 64 + rim_lane[(py, pz)]
                    shifts[m // 2, row, col] = 1
    return faces, place, offsets, shifts


def nt_dot(a, b):
    return lax.dot_general(a, b, (((1,), (1,)), ((), ())), preferred_element_type=F32)


def tn_dot(a, b):
    return lax.dot_general(a, b, (((0,), (0,)), ((), ())), preferred_element_type=F32)


def dot(a, b):
    return jnp.dot(a, b, preferred_element_type=F32)


def below(rows, lane):
    return lax.broadcasted_iota(jnp.int32, (rows, 128), 1) < lane


def main_kernel(
    feat_hbm, k1_hbm, k2_hbm, occ_hbm, nb_hbm, cot_hbm, faces_hbm, place_hbm, offs_hbm, shift_hbm,
    out_ref, full1_ref, full2_ref,
    feat_ref, k1_ref, k2_ref, occ_ref, nb_ref, cot_ref, faces_ref, place_ref, offs_ref, shift_ref,
    sx_a, se_a, sz_a, rx_a, re_a, rz_a, sx_h, se_h, sz_h, rx_h, re_h, rz_h,
    src1, src2, ev1, od1, ev2, od2, evg, odg,
    pk1, pk2, sb1, sb2, rb1, rb2, b11, b12, r11, r12, b21, b22, r21, r22, t21, t22,
    b31, b32, t31, t32, r31, r32, f1, f2, send_sem, recv_sem, out_sem, in_sem,
):
    reg = lax.axis_index("region")
    s = lax.axis_index("split")
    core = lax.rem(reg, 2)
    y = lax.rem(lax.div(reg, 2), 4)
    x = lax.rem(lax.div(reg, 8), 4)
    zh = lax.div(reg, 32)
    z = zh * 2 + s

    def dev(core_, x_, y_, z_):
        return (((lax.div(z_, 2) * 4 + x_) * 4 + y_) * 2 + core_, lax.rem(z_, 2))

    m1 = x + (y - x) * core
    m2 = y + (x - y) * core
    m1_other = y + (x - y) * core
    partner = dev(1 - core, x, y, z)

    def along1(v):
        return dev(core, x + (v - x) * (1 - core), y + (v - y) * core, z)

    def along2(v):
        return dev(core, x + (v - x) * core, y + (v - y) * (1 - core), z)

    def along_z(v):
        return dev(core, x, y, v)

    up, down = lax.rem(reg + 1, 128), lax.rem(reg + 127, 128)
    halo_peers = ((up, s), (down, s), (up, 1 - s), (down, 1 - s), (reg, 1 - s))

    barrier = pltpu.get_barrier_semaphore()
    peers = list(halo_peers) + [partner]
    peers += [along1(lax.rem(m1 + d, 4)) for d in range(1, 4)]
    peers += [along2(lax.rem(m2 + d, 4)) for d in range(1, 4)]
    peers += [along_z(lax.rem(z + d, 8)) for d in range(1, 8)]
    for peer in peers:
        pl.semaphore_signal(barrier, inc=1, device_id=peer, device_id_type=MESH)

    loads = {}
    pairs = (
        ("occ", occ_hbm, occ_ref), ("feat", feat_hbm, feat_ref), ("faces", faces_hbm.at[s], faces_ref),
        ("cot", cot_hbm, cot_ref), ("nb", nb_hbm, nb_ref), ("offs", offs_hbm, offs_ref),
        ("place", place_hbm, place_ref), ("shift", shift_hbm, shift_ref),
        ("k1", k1_hbm, k1_ref), ("k2", k2_hbm, k2_ref),
    )
    for i, (name, src, dst) in enumerate(pairs):
        loads[name] = pltpu.make_async_copy(src, dst, in_sem.at[i])
        loads[name].start()

    started = []

    def copy(src, dst, i, peer):
        c = pltpu.make_async_remote_copy(
            src_ref=src, dst_ref=dst, send_sem=send_sem.at[i], recv_sem=recv_sem.at[i],
            device_id=peer, device_id_type=MESH,
        )
        c.start()
        started.append(c)
        return c

    lane8 = lax.broadcasted_iota(jnp.int32, (8, 128), 1)

    def pack_halo(own, rolled, channels, sx, se, sz):
        blocks, half = channels // C1, channels // 2
        lo = below(half, 64)
        mid = 0 if blocks == 1 else C1 // 2
        at = slice(mid, mid + half) if blocks == 2 else slice(0, half)
        picked = dot(own.astype(BF16), faces_ref[...])
        sx[0, at, :] = jnp.where(lo, own[:half, 0:128], rolled[half:, 0:128]).astype(BF16)
        sx[1, at, :] = jnp.where(lo, rolled[:half, 0:128], own[half:, 384:512]).astype(BF16)
        sz[at, :] = jnp.where(lo, picked[:half, 0:128], picked[half:, 0:128]).astype(BF16)
        for b in range(blocks):
            to = (b + blocks - 1) * 8
            for q in range(2):
                edge = jnp.zeros((8, 128), F32)
                for g in range(12):
                    rows = slice(b * C1 + g * 8, b * C1 + g * 8 + 8)
                    edge = jnp.where(lax.div(lane8, 8) == g, picked[rows, 128 + 128 * q : 256 + 128 * q], edge)
                se[q, to : to + 8, :] = edge.astype(BF16)

    def unpack_halo(channels, rx, re, rz):
        blocks, half = channels // C1, channels // 2
        lo = below(half, 64)
        mid = 0 if blocks == 1 else C1 // 2
        at = slice(mid, mid + half)
        above, under, face = rx[0, at, :].astype(F32), rx[1, at, :].astype(F32), rz[at, :].astype(F32)
        planes = jnp.concatenate(
            [jnp.where(lo, above, pltpu.roll(under, 64, 1)), jnp.where(lo, pltpu.roll(above, 64, 1), under)], axis=0
        )
        face = jnp.concatenate([face, pltpu.roll(face, 64, 1)], axis=0)
        edges = []
        for b in range(blocks):
            rows = slice((b + blocks - 1) * 8, (b + blocks) * 8)
            above, under = re[0, rows, :].astype(F32), re[1, rows, :].astype(F32)
            for g in range(12):
                a = pltpu.roll(above, (64 - 8 * g) % 128, 1)
                u = pltpu.roll(under, (72 - 8 * g) % 128, 1)
                edges.append(jnp.where(lane8 < 72, a, u))
        side = jnp.where(below(channels, 64), face, jnp.concatenate(edges, axis=0))
        return jnp.concatenate([planes, side], axis=1).astype(BF16)

    def send_halo(sx, se, sz, rx, re, rz, base):
        return [
            copy(se.at[1], re.at[1], base, halo_peers[2]),
            copy(se.at[0], re.at[0], base + 1, halo_peers[3]),
            copy(sz, rz, base + 2, halo_peers[4]),
            copy(sx.at[1], rx.at[1], base + 3, halo_peers[0]),
            copy(sx.at[0], rx.at[0], base + 4, halo_peers[1]),
        ]

    loads["occ"].wait()
    loads["feat"].wait()
    loads["faces"].wait()
    active = (occ_ref[...] > 0).astype(F32)
    masked = feat_ref[...].astype(F32) * active
    masked_rolled = pltpu.roll(masked, 64, 1)
    pack_halo(masked, masked_rolled, C1, sx_a, se_a, sz_a)
    loads["cot"].wait()
    grad_wide = cot_ref[...].astype(F32) * active
    grad_rolled = pltpu.roll(grad_wide, 64, 1)
    pack_halo(grad_wide, grad_rolled, C2, sx_a, se_a, sz_a)
    grad_out = grad_wide.astype(BF16)
    loads["nb"].wait()
    loads["offs"].wait()
    present = (jnp.broadcast_to(nb_ref[...], (16, 27)) >= 0).astype(F32).astype(BF16)
    flags = dot(present, offs_ref[...])[0:1, :]

    pl.semaphore_wait(barrier, len(peers))
    halo_a = send_halo(sx_a, se_a, sz_a, rx_a, re_a, rz_a, 0)
    for name in ("place", "shift", "k1", "k2"):
        loads[name].wait()

    def gather(own, rolled, raw, channels, src, even, odd):
        lo = below(channels, 64)
        halo = dot(raw, place_ref[...]) * flags
        ends = halo[:, 0:128]
        halo = halo.astype(BF16)
        for j in range(9):
            t = j // 2
            if j % 2:
                inner = own[:, t * 128 : (t + 1) * 128]
                rim = halo[:, 768 + t * 128 : 896 + t * 128]
            else:
                inner = rolled[:, (t % 4) * 128 : (t % 4 + 1) * 128]
                if t == 0:
                    inner = jnp.where(lo, ends, inner)
                elif t == 4:
                    inner = jnp.where(lo, inner, ends)
                rim = halo[:, 128 + t * 128 : 256 + t * 128]
            src[j * channels : (j + 1) * channels, 0:128] = inner.astype(BF16)
            src[j * channels : (j + 1) * channels, 128:256] = rim

        def step(i, carry):
            moved = dot(src[...], shift_ref[i]).astype(BF16)
            for half in range(2):
                at = pl.ds(pl.multiple_of((2 * i + half) * channels, channels), channels)
                for j in range(9):
                    piece = moved[j * channels : (j + 1) * channels, half * 128 : (half + 1) * 128]
                    t = j // 2
                    if j % 2:
                        even[at, t * 128 : (t + 1) * 128] = piece
                    else:
                        odd[at, t * 128 : (t + 1) * 128] = piece
            return carry

        lax.fori_loop(0, 5, step, 0)

    def group(even, odd, rows, dx):
        if dx == 1:
            return even[rows, :]
        return odd[rows, 0:512] if dx == 0 else odd[rows, 128:640]

    first9 = slice(0, K9)

    def convolve(weights, even, odd):
        total = tn_dot(weights(0), group(even, odd, first9, 0))
        total += tn_dot(weights(1), group(even, odd, first9, 1))
        total += tn_dot(weights(2), group(even, odd, first9, 2))
        return total * active

    for c in halo_a:
        c.wait_recv()
    gather(masked, masked_rolled, unpack_halo(C1, rx_a, re_a, rz_a), C1, src1, ev1, od1)
    hidden_pre = convolve(lambda dx: k1_ref[dx * K9 : (dx + 1) * K9, :], ev1, od1)
    sig = jax.nn.sigmoid(hidden_pre)
    hidden = (hidden_pre * sig).astype(BF16).astype(F32)
    hidden_rolled = pltpu.roll(hidden, 64, 1)
    pack_halo(hidden, hidden_rolled, C1, sx_h, se_h, sz_h)
    halo_h = send_halo(sx_h, se_h, sz_h, rx_h, re_h, rz_h, 5)

    gather(grad_wide, grad_rolled, unpack_halo(C2, rx_a, re_a, rz_a), C2, src2, evg, odg)
    lo1296 = below(1296, 64)

    def reduce_steps(h, base, pk, sb, rb, b1, r1, b2, r2, t2, b3, t3, r3, full):
        q1, q2, q3 = h // 4, h // 16, h // 128
        order = (2, 1, 3, 0)
        half = pl.ds(pl.multiple_of((1 - core) * h, h), h)
        sb[...] = pk[half, :].astype(BF16).reshape(4, q1, 128)
        first = []
        for n, d in enumerate(order):
            v = lax.rem(m1_other + d, 4)
            first.append(copy(sb.at[v], rb.at[n], base + n, partner))
        yield
        own = None
        second = []
        for n, d in enumerate(order):
            first[n].wait_recv()
            v = lax.rem(m1 + d, 4)
            part = pk[pl.ds(pl.multiple_of(core * h + v * q1, q1), q1), :] + rb[n].astype(F32)
            if d:
                b1[d - 1] = part.astype(BF16)
                second.append(copy(b1.at[d - 1], r1.at[d - 1], base + 3 + d, along1(v)))
            else:
                own = part
        yield
        for c in second:
            c.wait_recv()
        own = own + r1[0].astype(F32) + r1[1].astype(F32) + r1[2].astype(F32)
        b2[...] = own.reshape(4, q2, 128)
        third = []
        for d in (2, 1, 3):
            v = lax.rem(m2 + d, 4)
            t2[d - 1] = b2[v].astype(BF16)
            third.append(copy(t2.at[d - 1], r2.at[d - 1], base + 6 + d, along2(v)))
        yield
        for c in third:
            c.wait_recv()
        own = b2[m2] + r2[0].astype(F32) + r2[1].astype(F32) + r2[2].astype(F32)
        b3[...] = own.reshape(8, q3, 128)
        t3[...] = own.reshape(8, q3, 128).astype(BF16)
        fourth = []
        for d in (4, 3, 5, 2, 6, 1, 7):
            v = lax.rem(z + d, 8)
            fourth.append(copy(t3.at[v], r3.at[d - 1], base + 9 + d, along_z(v)))
        yield
        for c in fourth:
            c.wait_recv()
        own = b3[z]
        for d in range(7):
            own = own + r3[d].astype(F32)
        full[core, m1, m2, z] = own.astype(BF16)
        mine = full.at[core, m1, m2, z]
        fifth = []
        for d in (4, 3, 5, 2, 6, 1, 7):
            v = lax.rem(z + d, 8)
            fifth.append(copy(mine, mine, base + 16 + d, along_z(v)))
        yield
        for c in fifth:
            c.wait_recv()
        mine = full.at[core, m1, m2]
        sixth = []
        for d in (2, 1, 3):
            v = lax.rem(m2 + d, 4)
            sixth.append(copy(mine, mine, base + 23 + d, along2(v)))
        yield
        for c in sixth:
            c.wait_recv()
        seventh = []
        for d in (2, 1, 3):
            v = lax.rem(m1 + d, 4)
            seventh.append(copy(full.at[core, m1], full.at[core, m1], base + 26 + d, along1(v)))
        eighth = [copy(full.at[core, m1], full.at[core, m1], base + 30, partner)]
        yield
        for n, d in ((1, 1), (2, 3), (0, 2)):
            seventh[n].wait_recv()
            v = lax.rem(m1 + 4 - d, 4)
            eighth.append(copy(full.at[core, v], full.at[core, v], base + 30 + d, partner))
        yield
        for c in eighth:
            c.wait_recv()
        yield

    red1 = reduce_steps(SEGS[0], 10, pk1, sb1, rb1, b11, r11, b21, r21, t21, b31, t31, r31, f1)
    red2 = reduce_steps(SEGS[1], 44, pk2, sb2, rb2, b12, r12, b22, r22, t22, b32, t32, r32, f2)

    for c in halo_h:
        c.wait_recv()
    gather(hidden, hidden_rolled, unpack_halo(C1, rx_h, re_h, rz_h), C1, src1, ev2, od2)
    grad = jnp.concatenate(
        [nt_dot(group(ev2, od2, first9, dx), grad_out) for dx in range(3)], axis=0
    )
    pk2[0:2592, :] = grad[:, 0:128]
    tail = jnp.concatenate([grad[:, 128:192], jnp.zeros((2592, 64), F32)], axis=1)
    pk2[2592:3888, :] = jnp.where(lo1296, tail[0:1296], pltpu.roll(tail[1296:2592], 64, 1))
    pk2[3888:4096, :] = jnp.zeros((208, 128), F32)
    next(red2)

    back = jnp.zeros((C1, 512), F32)
    for dx in range(3):
        for m in range(9):
            back += dot(k2_ref[26 - 9 * dx - m], group(evg, odg, slice(m * C2, (m + 1) * C2), dx))
    grad_pre = back * sig * (1.0 + hidden_pre * (1.0 - sig)) * active
    grad_pre = jnp.concatenate([grad_pre, jnp.zeros((32, 512), F32)], axis=0).astype(BF16)
    next(red2)
    grad = jnp.concatenate(
        [nt_dot(group(ev1, od1, first9, dx), grad_pre) for dx in range(3)], axis=0
    )
    pk1[0:1296, :] = jnp.where(lo1296, grad[0:1296], pltpu.roll(grad[1296:2592], 64, 1))
    lane = lax.broadcasted_iota(jnp.int32, (648, 128), 1)
    rest = pltpu.roll(grad[0:648], 64, 1)
    for q in range(1, 4):
        rest = jnp.where(lane < 32 * q, rest, pltpu.roll(grad[648 * q : 648 * (q + 1)], (32 * q + 64) % 128, 1))
    pk1[1296:1944, :] = rest
    pk1[1944:2048, :] = jnp.zeros((104, 128), F32)
    next(red1)
    next(red1)
    out_ref[...] = convolve(
        lambda dx: k2_ref[9 * dx : 9 * dx + 9].reshape(K9, C2), ev2, od2
    ).astype(BF16)
    next(red2)
    next(red1)
    next(red2)
    next(red1)
    next(red2)
    next(red1)
    next(red2)
    next(red1)
    next(red2)
    next(red1)
    next(red2)
    next(red1)
    next(red2)
    save2 = pltpu.make_async_copy(f2, full2_ref, out_sem.at[1])
    save2.start()
    next(red1)
    save1 = pltpu.make_async_copy(f1, full1_ref, out_sem.at[0])
    save1.start()
    for c in started:
        c.wait_send()
    save2.wait()
    save1.wait()


def unpack_kernel(
    p1_hbm, p2_hbm, o_hbm, g1_hbm, g2_hbm, out_hbm, p1_ref, p2_ref, o_ref, g1_ref, g2_ref, in_sem, out_sem
):
    loads = [
        pltpu.make_async_copy(src, dst, in_sem.at[i])
        for i, (src, dst) in enumerate(((p2_hbm, p2_ref), (p1_hbm, p1_ref), (o_hbm, o_ref)))
    ]
    for c in loads:
        c.start()
    stores = []

    def store(src, dst):
        stores.append(pltpu.make_async_copy(src, dst, out_sem.at[len(stores)]))
        stores[-1].start()

    loads[0].wait()
    for q in range(4):
        rows = slice(648 * q, 648 * (q + 1))
        g2_ref[rows, 0:128] = p2_ref[rows, :].astype(F32)
        fold = p2_ref[2592 + (q % 2) * 648 : 3240 + (q % 2) * 648, :].astype(F32)
        if q > 1:
            fold = pltpu.roll(fold, 64, 1)
        g2_ref[rows, 128:192] = fold[:, 0:64]
        store(g2_ref.at[rows], g2_hbm.at[rows])
    loads[1].wait()
    lo = below(648, 64)
    for q in range(4):
        rows = slice(648 * q, 648 * (q + 1))
        left = p1_ref[(q % 2) * 648 : (q % 2 + 1) * 648, :].astype(F32)
        if q > 1:
            left = pltpu.roll(left, 64, 1)
        right = pltpu.roll(p1_ref[1296:1944, :].astype(F32), (64 - 32 * q) % 128, 1)
        g1_ref[rows, :] = jnp.where(lo, left, right)[:, 0:96]
        store(g1_ref.at[rows], g1_hbm.at[rows])
    loads[2].wait()
    store(o_ref, out_hbm)
    for c in stores:
        c.wait()


def shards(features, kernel_one, kernel_two, occupancy, neighbors, cotangent):
    faces, place, offsets, shifts = (jnp.asarray(a, BF16) for a in one_hots())
    hbm, any_ = pl.BlockSpec(memory_space=pltpu.HBM), pl.BlockSpec(memory_space=pl.ANY)
    vmem = pl.BlockSpec(memory_space=pltpu.VMEM)

    def reduce_scratch(h):
        q1, q2, q3 = h // 4, h // 16, h // 128
        return [
            pltpu.VMEM((2 * h, 128), F32),
            pltpu.VMEM((4, q1, 128), BF16),
            pltpu.VMEM((4, q1, 128), BF16),
            pltpu.VMEM((3, q1, 128), BF16),
            pltpu.VMEM((3, q1, 128), BF16),
            pltpu.VMEM((4, q2, 128), F32),
            pltpu.VMEM((3, q2, 128), BF16),
            pltpu.VMEM((3, q2, 128), BF16),
            pltpu.VMEM((8, q3, 128), F32),
            pltpu.VMEM((8, q3, 128), BF16),
            pltpu.VMEM((7, q3, 128), BF16),
            pltpu.VMEM((2, 4, 4, 8, q3, 128), BF16),
        ]

    pairs = zip(reduce_scratch(SEGS[0]), reduce_scratch(SEGS[1]))
    rows = 10 * C1

    def halo_scratch(channels):
        half, edge = channels // 2, channels // 12
        return 2 * [
            pltpu.VMEM((2, half, 128), BF16),
            pltpu.VMEM((2, edge, 128), BF16),
            pltpu.VMEM((half, 128), BF16),
        ]

    scratch = [
        pltpu.VMEM((C1, 512), BF16),
        pltpu.VMEM((27 * C1, C1), BF16),
        pltpu.VMEM((27, C1, C2), BF16),
        pltpu.VMEM((1, 512), jnp.int32),
        pltpu.VMEM((1, 27), jnp.int32),
        pltpu.VMEM((C2, 512), BF16),
        pltpu.VMEM((512, 384), BF16),
        pltpu.VMEM((256, 1280), BF16),
        pltpu.VMEM((27, 1280), BF16),
        pltpu.VMEM((5, 256, 256), BF16),
        *halo_scratch(C1 + C2),
        *halo_scratch(C1),
        pltpu.VMEM((9 * C1, 256), BF16),
        pltpu.VMEM((9 * C2, 256), BF16),
        pltpu.VMEM((rows, 512), BF16),
        pltpu.VMEM((rows, 640), BF16),
        pltpu.VMEM((rows, 512), BF16),
        pltpu.VMEM((rows, 640), BF16),
        pltpu.VMEM((2 * rows, 512), BF16),
        pltpu.VMEM((2 * rows, 640), BF16),
        *(ref for pair in pairs for ref in pair),
        pltpu.SemaphoreType.DMA((NCOPY,)),
        pltpu.SemaphoreType.DMA((NCOPY,)),
        pltpu.SemaphoreType.DMA((2,)),
        pltpu.SemaphoreType.DMA((10,)),
    ]
    out, full1, full2 = pl.pallas_call(
        main_kernel,
        out_shape=(
            jax.ShapeDtypeStruct((C2, 512), BF16),
            jax.ShapeDtypeStruct((2, 4, 4, 8, SEGS[0] // 128, 128), BF16),
            jax.ShapeDtypeStruct((2, 4, 4, 8, SEGS[1] // 128, 128), BF16),
        ),
        in_specs=[hbm] * 10,
        out_specs=(vmem, any_, any_),
        scratch_shapes=scratch,
        compiler_params=pltpu.CompilerParams(
            collective_id=0, has_side_effects=True, vmem_limit_bytes=VMEM_MIB << 20
        ),
        name="sparse_conv",
    )(
        *(
            pltpu.with_memory_space_constraint(a, pltpu.HBM)
            for a in (
                features, kernel_one.reshape(27 * C1, C1), kernel_two,
                occupancy, neighbors, cotangent, faces, place, offsets, shifts,
            )
        )
    )
    grad_one, grad_two, out = pl.pallas_call(
        unpack_kernel,
        out_shape=(
            jax.ShapeDtypeStruct((27 * C1, C1), F32),
            jax.ShapeDtypeStruct((27 * C1, C2), F32),
            jax.ShapeDtypeStruct((C2, 512), BF16),
        ),
        in_specs=[any_] * 3,
        out_specs=[hbm] * 3,
        scratch_shapes=[
            pltpu.VMEM((2 * SEGS[0], 128), BF16),
            pltpu.VMEM((2 * SEGS[1], 128), BF16),
            pltpu.VMEM((C2, 512), BF16),
            pltpu.VMEM((27 * C1, C1), F32),
            pltpu.VMEM((27 * C1, C2), F32),
            pltpu.SemaphoreType.DMA((3,)),
            pltpu.SemaphoreType.DMA((9,)),
        ],
        compiler_params=pltpu.CompilerParams(vmem_limit_bytes=16 << 20),
        name="unpack",
    )(full1.reshape(2 * SEGS[0], 128), full2.reshape(2 * SEGS[1], 128), out)
    return (out, grad_one.reshape(27, C1, C1), grad_two.reshape(27, C1, C2))


def solution(mesh):
    in_specs = (
        P(None, ("region", "split")),
        P(),
        P(),
        P(("region", "split"), None),
        P(("region", "split"), None),
        P(None, ("region", "split")),
    )
    out_specs = (P(None, ("region", "split")), P(), P())
    return jax.shard_map(shards, mesh=mesh, in_specs=in_specs, out_specs=out_specs, check_vma=False)
```
